32 devices in a mesh: fsdp: 8 (over y, x, core), tp: 4 (over z).
Axes of the slice: x: 2, y: 2, z: 4, core: 2. Of those that a mesh axis runs over, the one named last changes fastest.
Arguments:
- inputs: bfloat16 [2, 8, 1024, 2048], P(None, 'fsdp', 'tp'), may hold values from -6 to 6
- cotangent: bfloat16 [2, 8, 1024, 2048], P(None, 'fsdp', 'tp'), may hold values from -6 to 6
- segment_ids: int32 [2, 8, 1024], P(None, 'fsdp'), may hold values from 0 to 2, as said below
- block_ids: int32 [2, 8, 1024], P(None, 'fsdp'), may hold values from 0 to 1, as said below
- positions: int32 [2, 8, 1024], P(None, 'fsdp'), may hold values from 0 to 511, as said below
- w_qkv: bfloat16 [2048, 3, 2048], P('fsdp', None, 'tp'), may hold values from -0.15625 to 0.15625
- w_out: bfloat16 [2048, 2048], P('fsdp', 'tp'), may hold values from -0.75 to 0.75
- w_gateup: bfloat16 [2048, 2, 8192], P('fsdp', None, 'tp'), may hold values from -0.125 to 0.125
- w_down: bfloat16 [2048, 8192], P('fsdp', 'tp'), may hold values from -0.125 to 0.125
- gain_attn: bfloat16 [2048], P('fsdp'), may hold values from 0.25 to 1.75
- gain_ffn: bfloat16 [2048], P('fsdp'), may hold values from 0.25 to 1.75
Outputs:
- outputs: bfloat16 [2, 8, 1024, 2048], P(None, 'fsdp', 'tp')
- grad_inputs: float32 [2, 8, 1024, 2048], P(None, 'fsdp', 'tp')
- grad_qkv: float32 [2048, 3, 2048], P('fsdp', None, 'tp')
- grad_out: float32 [2048, 2048], P('fsdp', 'tp')
- grad_gateup: float32 [2048, 2, 8192], P('fsdp', None, 'tp')
- grad_down: float32 [2048, 8192], P('fsdp', 'tp')
- grad_gain_attn: float32 [2048], P('fsdp')
- grad_gain_ffn: float32 [2048], P('fsdp')
The draws below stay inside these ranges and needn't reach their ends.
Inputs may be any that keep to these rules, and one draw needn't show every extreme that they name: `segment_ids`: each sequence holds 3 documents of one or more tokens, numbered in order from 0; the last one starts at token 512. `positions`: the token's offset from the first token of its document. `block_ids`: positions // 256.
All inputs are finite; a program needn't handle non-finite values.
Results may differ from the reference program's by a relative error of at most 0.015.
Values may be sent and summed in bfloat16 or wider, within the bound.
No kernel may reach another device: no remote copies, remote signals or barrier semaphores. Data moves between devices by JAX's collectives and lax.ppermute only.
A program may use at most 448 MiB of HBM per device.

```python
import math
import jax
import jax.numpy as jnp
from jax import lax

D = 2048
H = 16
HD = 128
FF = 8192
LEN = 1024
MICRO = 2
BLK = 256
DOCS = 3
SEQS = 8


def document_layout(key):
    folded = jax.random.fold_in(key, 1301)
    subkeys = jax.random.split(folded, MICRO * SEQS)
    ladder = jnp.arange(LEN, dtype=jnp.int32)
    last_start = jnp.full((1,), LEN // 2, dtype=jnp.int32)

    def single_layout(subkey):
        early_cuts = jnp.sort(jax.random.permutation(subkey, LEN // 2 - 1)[:DOCS - 2] + 1).astype(jnp.int32)
        cut_points = jnp.concatenate([early_cuts, last_start]).astype(jnp.int32)
        beyond_cut = ladder[:, None] >= cut_points[None, :]
        segment = jnp.sum(beyond_cut.astype(jnp.int32), axis=1).astype(jnp.int32)
        doc_start = jnp.max(jnp.where(beyond_cut, cut_points[None, :], 0), axis=1).astype(jnp.int32)
        return (segment, (ladder - doc_start).astype(jnp.int32))
    segment, offset = jax.vmap(single_layout)(subkeys)
    full_shape = (MICRO, SEQS, LEN)
    return (segment.reshape(full_shape).astype(jnp.int32), offset.reshape(full_shape).astype(jnp.int32))


def draw_segment_ids(key, part):
    return document_layout(key)[0]


def draw_positions(key, part):
    return document_layout(key)[1]


def draw_block_ids(key, part):
    return (document_layout(key)[1] // BLK).astype(jnp.int32)


def levels(rng, dims, pieces, least, high):
    def one(axis_at, shards_of):
        draws = jax.random.uniform(jax.random.fold_in(jax.random.fold_in(rng, 6), axis_at), (shards_of,), jnp.float32, least / len(pieces), high / len(pieces))
        return jnp.repeat(jnp.exp(draws), dims[axis_at] // shards_of).reshape((-1,) + (1,) * (len(dims) - axis_at - 1))

    factor_of = one(*pieces[0])
    for cut in pieces[1:]:
        factor_of = factor_of * one(*cut)
    return factor_of


def bell_draw(rng, shape, scale, most, cuts=(), kind=jnp.bfloat16):
    values = jax.random.normal(rng, shape, jnp.float32) * scale
    if len(cuts) > 0:
        values = levels(rng, shape, cuts, -0.22, 0.18) * values
    return jnp.clip(values, min=-most, max=most).astype(kind)


def setup_inputs(seed: int = 0) -> dict:
    arg_keys = jax.random.split(jax.random.key(seed), 12)
    return {
        "inputs": bell_draw(arg_keys[0], (MICRO, SEQS, LEN, D), 1.0, 6.0, ((1, 8), (2, 4))),
        "cotangent": bell_draw(arg_keys[1], (MICRO, SEQS, LEN, D), 1.0, 6.0, ((1, 8), (2, 4))),
        "segment_ids": draw_segment_ids(jax.random.fold_in(arg_keys[11], 71), 0),
        "block_ids": draw_block_ids(jax.random.fold_in(arg_keys[11], 71), 0),
        "positions": draw_positions(jax.random.fold_in(arg_keys[11], 71), 0),
        "w_qkv": bell_draw(arg_keys[5], (D, 3, D), (D * 2 // 3) ** -0.5, 0.15625, ((0, 8), (2, 4))),
        "w_out": bell_draw(arg_keys[6], (D, D), (D // 32) ** -0.5, 0.75, ((0, 8), (1, 4))),
        "w_gateup": bell_draw(arg_keys[7], (D, 2, FF), D ** -0.5, 0.125, ((0, 8), (2, 4))),
        "w_down": bell_draw(arg_keys[8], (D, FF), (FF // 4) ** -0.5, 0.125, ((0, 8), (1, 4))),
        "gain_attn": jnp.clip(1.0 + 0.15 * jax.random.normal(arg_keys[9], (D,), jnp.float32), 0.25, 1.75).astype(jnp.bfloat16),
        "gain_ffn": jnp.clip(1.0 + 0.15 * jax.random.normal(arg_keys[10], (D,), jnp.float32), 0.25, 1.75).astype(jnp.bfloat16),
    }


@jax.custom_vjp
def low(v):
    return lax.optimization_barrier(v.astype(jnp.bfloat16)).astype(jnp.float32)

@jax.custom_vjp
def low_back(v):
    return v

def low_keep(v):
    return (low(v), None)

def low_pass(kept, grad):
    return (grad,)

def back_keep(v):
    return (v, None)

def back_low(kept, grad):
    return (low(grad),)
low.defvjp(low_keep, low_pass)
low_back.defvjp(back_keep, back_low)
eps_norm = 1e-06
rope_base = 10000.0

def rope_tables(positions, half_size):
    ladder = jnp.arange(half_size, dtype=jnp.float32) * (1.0 / half_size)
    frequency = jnp.exp(-math.log(rope_base) * ladder)
    angles = positions.astype(jnp.float32)[:, None] * frequency[None, :]
    return (jnp.cos(angles)[:, None, :], jnp.sin(angles)[:, None, :])

def rotate(values, cosine, sine):
    half_size = values.shape[-1] // 2
    first_half = values[..., :half_size]
    second_half = values[..., half_size:]
    return jnp.concatenate([first_half * cosine - second_half * sine, second_half * cosine + first_half * sine], axis=-1)

def normalize(values):
    return values * lax.rsqrt(lax.optimization_barrier(jnp.mean(values * values, axis=-1, keepdims=True)) + eps_norm)

def product(form, left, right):
    return jnp.einsum(form, left, right, precision=lax.Precision.HIGHEST)

def one_sequence(params, tokens, seg_here, blk_here, pos_here):
    weight_qkv, weight_out, weight_gateup, weight_down, gain_one, gain_two = params
    length = tokens.shape[0]
    normed_one = low(normalize(tokens) * gain_one)
    projected = low_back(product('td,dce->tce', normed_one, weight_qkv))
    cosine, sine = rope_tables(pos_here, HD // 2)
    query = low(rotate(projected[:, 0].reshape(length, H, HD), cosine, sine))
    keys = low(rotate(projected[:, 1].reshape(length, H, HD), cosine, sine))
    values = low(projected[:, 2].reshape(length, H, HD))
    scores = low_back(product('qhd,khd->hqk', query, keys) * (1.0 / math.sqrt(HD)) - math.log(length))
    allowed = (seg_here[:, None] == seg_here[None, :]) & (blk_here[None, :] <= blk_here[:, None])
    weights = low(jnp.where(allowed[None], jax.nn.sigmoid(scores), 0.0))
    mixed = low(low_back(product('hqk,khd->qhd', weights, values).reshape(length, D)))
    attention = low_back(product('tc,dc->td', mixed, weight_out))
    middle = tokens + attention
    normed_two = low(normalize(middle) * gain_two)
    gate_up = low_back(product('td,dce->tce', normed_two, weight_gateup))
    hidden = low(jax.nn.silu(gate_up[:, 0]) * gate_up[:, 1])
    branch = low_back(product('tf,df->td', hidden, weight_down))
    return middle + branch

def reference(inputs, cotangent, segment_ids, block_ids, positions, w_qkv, w_out, w_gateup, w_down, gain_attn, gain_ffn):
    total = MICRO * SEQS
    params = tuple((weight.astype(jnp.float32) for weight in (w_qkv, w_out, w_gateup, w_down, gain_attn, gain_ffn)))
    tokens_all = inputs.reshape(total, LEN, D).astype(jnp.float32)
    seg_all = segment_ids.reshape(total, LEN)
    blk_all = block_ids.reshape(total, LEN)
    pos_all = positions.reshape(total, LEN)

    def forward(params, tokens_all):

        def step(carry, item):
            tokens, seg_here, blk_here, pos_here = item
            return (carry, jax.checkpoint(one_sequence)(params, tokens, seg_here, blk_here, pos_here))
        _, results = lax.scan(step, jnp.zeros((), jnp.float32), (tokens_all, seg_all, blk_all, pos_all))
        return results
    results, pullback = jax.vjp(forward, params, tokens_all)
    grads, grad_tokens = pullback(cotangent.reshape(total, LEN, D).astype(jnp.float32))
    outputs = results.reshape(MICRO, SEQS, LEN, D).astype(jnp.bfloat16)
    grad_inputs = grad_tokens.reshape(MICRO, SEQS, LEN, D)
    return (outputs, grad_inputs, grads[0], grads[1], grads[2], grads[3], grads[4], grads[5])
```

```python
import math

import jax
import jax.numpy as jnp
from jax import lax
from jax.experimental import pallas as pl
from jax.experimental.pallas import tpu as pltpu
from jax.sharding import PartitionSpec as P

HD = 128


eps_norm = 1e-06
rope_base = 10000.0


def rope_tables(positions, half_size):
    ladder = jnp.arange(half_size, dtype=jnp.float32) * (1.0 / half_size)
    frequency = jnp.exp(-math.log(rope_base) * ladder)
    angles = positions.astype(jnp.float32)[:, None] * frequency[None, :]
    return (jnp.cos(angles)[:, None, :], jnp.sin(angles)[:, None, :])


def rotate(values, cosine, sine):
    half_size = values.shape[-1] // 2
    first_half = values[..., :half_size]
    second_half = values[..., half_size:]
    return jnp.concatenate(
        [first_half * cosine - second_half * sine, second_half * cosine + first_half * sine],
        axis=-1,
    )


def rotate_back(grads, cosine, sine):
    half_size = grads.shape[-1] // 2
    first_half = grads[..., :half_size]
    second_half = grads[..., half_size:]
    return jnp.concatenate(
        [first_half * cosine + second_half * sine, second_half * cosine - first_half * sine],
        axis=-1,
    )


def normalize(values):
    factor = lax.rsqrt(jnp.mean(values * values, axis=-1, keepdims=True) + eps_norm)
    return (values * factor, factor)


def normalize_back(grad_normed, unit, factor, gain):
    grad_unit = grad_normed * gain
    return factor * (grad_unit - unit * jnp.mean(grad_unit * unit, axis=-1, keepdims=True))


def visible(seg_query, blk_query, seg_keys, blk_keys):
    return (seg_query[:, None] == seg_keys[None, :]) & (blk_keys[None, :] <= blk_query[:, None])


def score_block(query_block, keys, shift):
    scale = 1.0 / math.sqrt(keys.shape[-1])
    return (
        jnp.einsum("qhd,khd->hqk", query_block, keys, preferred_element_type=jnp.float32) * scale
        + shift
    )


def attend(query, keys, values, seg_here, blk_here, shift):
    length, heads, size = query.shape
    block_rows = min(length, 512)
    blocks = length // block_rows
    query_blocks = query.reshape(blocks, block_rows, heads, size)
    seg_blocks = seg_here.reshape(blocks, block_rows)
    blk_blocks = blk_here.reshape(blocks, block_rows)

    def single_block(item):
        query_block, seg_block, blk_block = item
        scores = score_block(query_block, keys, shift)
        allowed = visible(seg_block, blk_block, seg_here, blk_here)
        weights = jnp.where(allowed[None], jax.nn.sigmoid(scores), 0.0).astype(jnp.bfloat16)
        return jnp.einsum("hqk,khd->qhd", weights, values, preferred_element_type=jnp.float32)

    mixed = lax.map(single_block, (query_blocks, seg_blocks, blk_blocks))
    return mixed.reshape(length, heads * size).astype(jnp.bfloat16)


def attend_back(query, keys, values, grad_mixed, seg_here, blk_here, shift):
    length, heads, size = query.shape
    scale = 1.0 / math.sqrt(size)
    block_rows = min(length, 512)
    blocks = length // block_rows
    query_blocks = query.reshape(blocks, block_rows, heads, size)
    grad_blocks = grad_mixed.reshape(blocks, block_rows, heads, size)
    seg_blocks = seg_here.reshape(blocks, block_rows)
    blk_blocks = blk_here.reshape(blocks, block_rows)

    def single_block(carry, item):
        grad_keys, grad_values = carry
        query_block, grad_block, seg_block, blk_block = item
        scores = score_block(query_block, keys, shift)
        allowed = visible(seg_block, blk_block, seg_here, blk_here)
        sigma = jax.nn.sigmoid(scores)
        weights = jnp.where(allowed[None], sigma, 0.0).astype(jnp.bfloat16)
        grad_weights = jnp.einsum(
            "qhd,khd->hqk", grad_block, values, preferred_element_type=jnp.float32
        )
        grad_scores = jnp.where(allowed[None], grad_weights * sigma * (1.0 - sigma), 0.0).astype(
            jnp.bfloat16
        )
        grad_values = grad_values + jnp.einsum(
            "hqk,qhd->khd", weights, grad_block, preferred_element_type=jnp.float32
        )
        grad_keys = (
            grad_keys
            + jnp.einsum(
                "hqk,qhd->khd", grad_scores, query_block, preferred_element_type=jnp.float32
            )
            * scale
        )
        grad_query = (
            jnp.einsum("hqk,khd->qhd", grad_scores, keys, preferred_element_type=jnp.float32)
            * scale
        )
        return ((grad_keys, grad_values), grad_query)

    zeros = jnp.zeros((length, heads, size), jnp.float32)
    (grad_keys, grad_values), grad_query = lax.scan(
        single_block, (zeros, zeros), (query_blocks, grad_blocks, seg_blocks, blk_blocks)
    )
    return (grad_query.reshape(length, heads, size), grad_keys, grad_values)


def grad_rows(saved, count):
    total = None
    for (
        normed_full,
        grad_qkv,
        grad_middle_full,
        mixed,
        normed_two_full,
        grad_gu,
        grad_top_full,
        hidden,
    ) in saved:
        term_qkv = jnp.einsum(
            "td,tce->dce", normed_full, grad_qkv, preferred_element_type=jnp.float32
        ).reshape(count, -1)
        term_out = jnp.einsum(
            "td,tc->dc", grad_middle_full, mixed, preferred_element_type=jnp.float32
        )
        term_gu = jnp.einsum(
            "td,tce->dce", normed_two_full, grad_gu, preferred_element_type=jnp.float32
        ).reshape(count, -1)
        term_down = jnp.einsum(
            "td,tf->df", grad_top_full, hidden, preferred_element_type=jnp.float32
        )
        joined = jnp.concatenate([term_qkv, term_out, term_gu, term_down], axis=1)
        total = joined
    return total


def local(
    inputs,
    cotangent,
    segment_ids,
    block_ids,
    positions,
    w_qkv,
    w_out,
    w_gateup,
    w_down,
    gain_attn,
    gain_ffn,
):
    micro = inputs.shape[0]
    local_rows = inputs.shape[2]
    width = inputs.shape[3]
    length = segment_ids.shape[2]
    shard_rows = w_qkv.shape[0]
    width_here = w_qkv.shape[2]
    hidden_here = w_gateup.shape[2]
    heads_here = width_here // HD
    shift = -math.log(length)
    results = []
    grad_results = []
    summed = None
    gain_one_total = jnp.zeros((width,), jnp.float32)
    gain_two_total = jnp.zeros((width,), jnp.float32)
    for batch_index in range(micro):
        qkv_full, out_full, gain_one = (
            lax.all_gather(w_qkv, "fsdp", axis=0, tiled=True),
            lax.all_gather(w_out, "fsdp", axis=0, tiled=True),
            lax.all_gather(gain_attn, "fsdp", axis=0, tiled=True),
        )
        gateup_full, down_full, gain_two = (
            lax.all_gather(w_gateup, "fsdp", axis=0, tiled=True),
            lax.all_gather(w_down, "fsdp", axis=0, tiled=True),
            lax.all_gather(gain_ffn, "fsdp", axis=0, tiled=True),
        )
        gain_one = gain_one.astype(jnp.float32)
        gain_two = gain_two.astype(jnp.float32)
        seg_here = segment_ids[batch_index, 0]
        blk_here = block_ids[batch_index, 0]
        cosine, sine = rope_tables(positions[batch_index, 0], HD // 2)
        residual = inputs[batch_index, 0].astype(jnp.float32)
        unit_one, factor_one = normalize(residual)
        normed_one = (unit_one * gain_one).astype(jnp.bfloat16)
        normed_full = lax.all_gather(normed_one, "tp", axis=0, tiled=True)
        projected = jnp.einsum(
            "td,dce->tce", normed_full, qkv_full, preferred_element_type=jnp.float32
        )
        query = rotate(projected[:, 0].reshape(length, heads_here, HD), cosine, sine).astype(
            jnp.bfloat16
        )
        keys = rotate(projected[:, 1].reshape(length, heads_here, HD), cosine, sine).astype(
            jnp.bfloat16
        )
        values = projected[:, 2].reshape(length, heads_here, HD).astype(jnp.bfloat16)
        mixed = attend(query, keys, values, seg_here, blk_here, shift)

        def attn_term(start, count, mixed=mixed, out_full=out_full):
            return jnp.einsum("tc,dc->td", mixed, out_full, preferred_element_type=jnp.float32)

        middle = residual + lax.psum_scatter(
            attn_term(jnp.int32(0), local_rows * lax.axis_size("tp")),
            "tp",
            scatter_dimension=0,
            tiled=True,
        )
        unit_two, factor_two = normalize(middle)
        normed_two = (unit_two * gain_two).astype(jnp.bfloat16)
        normed_two_full = lax.all_gather(normed_two, "tp", axis=0, tiled=True)
        gate_up = jnp.einsum(
            "td,dce->tce", normed_two_full, gateup_full, preferred_element_type=jnp.float32
        )
        gate = gate_up[:, 0]
        up_part = gate_up[:, 1]
        gate_sigma = jax.nn.sigmoid(gate)
        gate_silu = gate * gate_sigma
        hidden = (gate_silu * up_part).astype(jnp.bfloat16)

        def ffn_term(start, count, hidden=hidden, down_full=down_full):
            return jnp.einsum("tf,df->td", hidden, down_full, preferred_element_type=jnp.float32)

        results.append(
            (
                middle
                + lax.psum_scatter(
                    ffn_term(jnp.int32(0), local_rows * lax.axis_size("tp")),
                    "tp",
                    scatter_dimension=0,
                    tiled=True,
                )
            ).astype(jnp.bfloat16)
        )
        grad_top = cotangent[batch_index, 0]
        grad_top_full = lax.all_gather(grad_top, "tp", axis=0, tiled=True)
        grad_hidden = jnp.einsum(
            "td,df->tf", grad_top_full, down_full, preferred_element_type=jnp.float32
        )
        grad_gate = grad_hidden * up_part * gate_sigma * (1.0 + gate * (1.0 - gate_sigma))
        grad_up = grad_hidden * gate_silu
        grad_gu = jnp.stack([grad_gate, grad_up], axis=1).astype(jnp.bfloat16)

        def ffn_back_term(start, count, grad_gu=grad_gu, gateup_full=gateup_full):
            return jnp.einsum(
                "tce,dce->td", grad_gu, gateup_full, preferred_element_type=jnp.float32
            )

        grad_normed_two = lax.psum_scatter(
            ffn_back_term(jnp.int32(0), local_rows * lax.axis_size("tp")),
            "tp",
            scatter_dimension=0,
            tiled=True,
        )
        grad_middle = grad_top.astype(jnp.float32) + normalize_back(
            grad_normed_two, unit_two, factor_two, gain_two
        )
        gain_two_total = gain_two_total + jnp.sum(grad_normed_two * unit_two, axis=0)
        grad_middle_full = lax.all_gather(
            grad_middle.astype(jnp.bfloat16), "tp", axis=0, tiled=True
        )
        grad_mixed = jnp.einsum(
            "td,dc->tc", grad_middle_full, out_full, preferred_element_type=jnp.float32
        ).astype(jnp.bfloat16)
        grad_query, grad_keys, grad_values = attend_back(
            query,
            keys,
            values,
            grad_mixed.reshape(length, heads_here, HD),
            seg_here,
            blk_here,
            shift,
        )
        grad_qkv = jnp.stack(
            [
                rotate_back(grad_query, cosine, sine).reshape(length, width_here),
                rotate_back(grad_keys, cosine, sine).reshape(length, width_here),
                grad_values.reshape(length, width_here),
            ],
            axis=1,
        ).astype(jnp.bfloat16)

        def attn_back_term(start, count, grad_qkv=grad_qkv, qkv_full=qkv_full):
            return jnp.einsum("tce,dce->td", grad_qkv, qkv_full, preferred_element_type=jnp.float32)

        grad_normed_one = lax.psum_scatter(
            attn_back_term(jnp.int32(0), local_rows * lax.axis_size("tp")),
            "tp",
            scatter_dimension=0,
            tiled=True,
        )
        grad_results.append(
            grad_middle + normalize_back(grad_normed_one, unit_one, factor_one, gain_one)
        )
        gain_one_total = gain_one_total + jnp.sum(grad_normed_one * unit_one, axis=0)
        record = (
            normed_full,
            grad_qkv,
            grad_middle_full,
            mixed,
            normed_two_full,
            grad_gu,
            grad_top_full,
            hidden,
        )
        batch_sum = lax.psum_scatter(
            grad_rows([record], shard_rows * lax.axis_size("fsdp")),
            "fsdp",
            scatter_dimension=0,
            tiled=True,
        )
        summed = batch_sum if summed is None else summed + batch_sum
    edge_one = 3 * width_here
    edge_two = 4 * width_here
    edge_three = edge_two + 2 * hidden_here
    grad_qkv_rows = summed[:, :edge_one].reshape(shard_rows, 3, width_here)
    grad_out_rows = summed[:, edge_one:edge_two]
    grad_gateup_rows = summed[:, edge_two:edge_three].reshape(shard_rows, 2, hidden_here)
    grad_down_rows = summed[:, edge_three:]
    gain_totals = lax.psum((gain_one_total, gain_two_total), ("fsdp", "tp"))
    first_row = lax.axis_index("fsdp") * shard_rows
    grad_gain_one = lax.dynamic_slice_in_dim(gain_totals[0], first_row, shard_rows, 0)
    grad_gain_two = lax.dynamic_slice_in_dim(gain_totals[1], first_row, shard_rows, 0)
    outputs = jnp.stack(results)[:, None]
    grad_inputs = jnp.stack(grad_results)[:, None]
    return (
        outputs,
        grad_inputs,
        grad_qkv_rows,
        grad_out_rows,
        grad_gateup_rows,
        grad_down_rows,
        grad_gain_one,
        grad_gain_two,
    )


QUADS = 4


def plane_fits(mesh):
    return mesh.shape["fsdp"] == 2 * QUADS and mesh.shape["tp"] == 4


def flips(size, bit):
    return [(index, index ^ bit) for index in range(size)]


def over_quad(value, step):
    return lax.ppermute(value, "fsdp", flips(2 * QUADS, 2 * step))


def over_core(value):
    return lax.ppermute(value, "fsdp", flips(2 * QUADS, 1))


def over_pair(value):
    return lax.ppermute(value, "tp", flips(lax.axis_size("tp"), 1))


def ring_up(value):
    size = lax.axis_size("tp")
    return lax.ppermute(value, "tp", [(index, (index + 1) % size) for index in range(size)])


def ring_down(value):
    size = lax.axis_size("tp")
    return lax.ppermute(value, "tp", [(index, (index - 1) % size) for index in range(size)])


def low(value):
    return value.astype(jnp.bfloat16)


def wide(value):
    return value.astype(jnp.float32)


def mm(form, left, right):
    return jnp.einsum(form, left, right, preferred_element_type=jnp.float32)


def choose(first, when_true, when_false):
    return jnp.where(first, when_true, when_false)


def spread_rows(weight, quad):
    rows, columns = weight.shape
    part = columns // QUADS
    pieces = [lax.dynamic_slice(weight, (0, quad * part), (rows, part))]
    for step in range(1, QUADS):
        piece = lax.dynamic_slice(weight, (0, (quad ^ step) * part), (rows, part))
        pieces.append(over_quad(piece, step))
    odd = (quad & 1) == 1
    high = (quad & 2) == 2
    ordered = []
    for index in range(QUADS):
        even_side = choose(odd, pieces[index ^ 1], pieces[index])
        far_side = choose(odd, pieces[index ^ 3], pieces[index ^ 2])
        ordered.append(choose(high, far_side, even_side))
    return jnp.stack(ordered)


def gather_columns(block, core):
    pieces = [block]
    for _ in range(lax.axis_size("tp") - 1):
        pieces.append(ring_up(pieces[-1]))
    whole = []
    first = core == 0
    quads, rows, part = block.shape
    for piece in pieces:
        other = over_core(piece)
        even_rows = choose(first, piece, other)
        odd_rows = choose(first, other, piece)
        whole.append(jnp.stack([even_rows, odd_rows], axis=1).reshape(2 * quads * rows, part))
    return jnp.concatenate(whole, axis=1)


def gather_tokens(own):
    half = own.shape[0] // 2
    from_x = over_quad(own, 1)
    from_y = over_quad(own, 2)
    far_top = over_quad(from_y[:half], 1)
    far_bottom = over_quad(from_x[half:], 2)
    return jnp.concatenate([own, from_x, from_y, far_top, far_bottom], axis=0)


def scatter_tokens(partial):
    count = partial.shape[0] // QUADS
    half = count // 2
    here, to_x, to_y, far = [partial[index * count : (index + 1) * count] for index in range(QUADS)]
    got_x = over_quad(low(jnp.concatenate([to_x[:half], far[:half]], axis=0)), 1)
    got_y = over_quad(low(jnp.concatenate([to_y[half:], far[half:]], axis=0)), 2)
    last_y = over_quad(low(wide(to_y[:half]) + wide(got_x[half:])), 2)
    last_x = over_quad(low(wide(to_x[half:]) + wide(got_y[half:])), 1)
    top = wide(here[:half]) + wide(got_x[:half]) + wide(last_y)
    bottom = wide(here[half:]) + wide(got_y[:half]) + wide(last_x)
    return jnp.concatenate([top, bottom], axis=0)


def reduce_weight_grad(grad, core, quad):
    size = lax.axis_size("tp")
    rows = grad.shape[0] // (2 * QUADS)
    part = grad.shape[1] // size
    split = grad.reshape(QUADS, 2, rows, size * part)
    first = core == 0
    keep = choose(first, split[:, 0], split[:, 1])
    send = low(choose(first, split[:, 1], split[:, 0]))
    got = over_core(send)
    total = keep + wide(got)
    running = total[:, :, (size - 1) * part :]
    for step in range(size - 2, -1, -1):
        running = total[:, :, step * part : (step + 1) * part] + wide(ring_down(low(running)))
    result = jnp.zeros((rows, QUADS * part), jnp.float32)
    for step in range(QUADS):
        piece = lax.dynamic_index_in_dim(running, quad ^ step, 0, keepdims=False)
        if step:
            piece = wide(over_quad(low(piece), step))
        result = lax.dynamic_update_slice(result, piece, (0, (quad ^ step) * part))
    return result


def reduce_gain_grads(sums, index):
    for bit in (4, 2, 1):
        count = sums.shape[1] // 2
        mine = (index & bit) // bit
        keep = lax.dynamic_slice_in_dim(sums, mine * count, count, 1)
        send = lax.dynamic_slice_in_dim(sums, (1 - mine) * count, count, 1)
        sums = keep + lax.ppermute(send, "fsdp", flips(2 * QUADS, bit))
    for bit in (1, 2):
        sums = sums + lax.ppermute(sums, "tp", flips(lax.axis_size("tp"), bit))
    return sums


def turn(values, cosine, sine):
    return values * cosine + pltpu.roll(values, values.shape[-1] // 2, 1) * sine


def turn_back(values, cosine, sine):
    return values * cosine - pltpu.roll(values, values.shape[-1] // 2, 1) * sine


def dot_nt(left, right):
    return lax.dot_general(
        left, right, (((1,), (1,)), ((), ())), preferred_element_type=jnp.float32
    )


def dot_tn(left, right):
    return lax.dot_general(
        left, right, (((0,), (0,)), ((), ())), preferred_element_type=jnp.float32
    )


def allowed_of(marks_row, marks_column):
    same = marks_column[0, :, 0:1] == marks_row[0, 0:1, :]
    seen = marks_row[0, 1:2, :] <= marks_column[0, :, 1:2]
    return jnp.where(same & seen, 1.0, 0.0)


def attention_kernel(
    shift, top, bottom, cosine, sine, marks_row, marks_column, qkv_out, mixed_out, allowed
):
    allowed[...] = allowed_of(marks_row, marks_column)
    heads = top.shape[1] // (3 * HD)
    count = top.shape[0]
    scale = 1.0 / math.sqrt(HD)
    for head in range(heads):
        parts = []
        for kind in range(3):
            at = (3 * head + kind) * HD
            values = jnp.concatenate([top[:, at : at + HD], bottom[:, at : at + HD]], axis=0)
            if kind < 2:
                values = turn(values, cosine[0], sine[0])
            values = values.astype(jnp.bfloat16)
            qkv_out[:, 0, :, at : at + HD] = values.reshape(2, count, HD)
            parts.append(values)
        query, keys, values = parts
        scores = dot_nt(query, keys) * scale + shift
        sigma = 1.0 / (1.0 + jnp.exp(-scores))
        weights = (sigma * allowed[...]).astype(jnp.bfloat16)
        mixed = jnp.dot(weights, values, preferred_element_type=jnp.float32)
        mixed_out[:, 0, :, head * HD : (head + 1) * HD] = mixed.astype(jnp.bfloat16).reshape(
            2, count, HD
        )


def attention_back_kernel(
    shift, qkv, grad_mixed, cosine, sine, marks_row, marks_column, grad_out, allowed
):
    allowed[...] = allowed_of(marks_row, marks_column)
    heads = qkv.shape[3] // (3 * HD)
    count = qkv.shape[2]
    scale = 1.0 / math.sqrt(HD)
    for head in range(heads):
        at = 3 * head * HD
        query, keys, values = [
            qkv[:, 0, :, at + kind * HD : at + (kind + 1) * HD].reshape(2 * count, HD)
            for kind in range(3)
        ]
        grads = grad_mixed[:, 0, :, head * HD : (head + 1) * HD].reshape(2 * count, HD)
        scores = dot_nt(query, keys) * scale + shift
        sigma = 1.0 / (1.0 + jnp.exp(-scores))
        kept = sigma * allowed[...]
        weights = kept.astype(jnp.bfloat16)
        grad_values = dot_tn(weights, grads)
        grad_scores = (dot_nt(grads, values) * kept * (1.0 - sigma)).astype(jnp.bfloat16)
        grad_query = jnp.dot(grad_scores, keys, preferred_element_type=jnp.float32) * scale
        grad_keys = dot_tn(grad_scores, query) * scale
        grad_query = turn_back(grad_query, cosine[0], sine[0])
        grad_keys = turn_back(grad_keys, cosine[0], sine[0])
        for kind, grad in enumerate((grad_query, grad_keys, grad_values)):
            grad_out[:, 0, :, at + kind * HD : at + (kind + 1) * HD] = grad.astype(
                jnp.bfloat16
            ).reshape(2, count, HD)


def token_block(count, columns):
    return pl.BlockSpec((2, 1, count, columns), lambda quad: (0, quad, 0, 0))


def piece_block(shape):
    return pl.BlockSpec((1,) + shape[1:], lambda quad: (quad, 0, 0))


def attention(top, bottom, cosine, sine, marks_row, marks_column, shift):
    count = top.shape[0] // QUADS
    columns = top.shape[1]
    width = columns // 3
    pairs = QUADS * (2 * count) * (2 * count) * (width // HD)
    return pl.pallas_call(
        lambda *refs: attention_kernel(shift, *refs),
        grid=(QUADS,),
        in_specs=[
            pl.BlockSpec((count, columns), lambda quad: (quad, 0)),
            pl.BlockSpec((count, columns), lambda quad: (quad, 0)),
            piece_block(cosine.shape),
            piece_block(sine.shape),
            piece_block(marks_row.shape),
            piece_block(marks_column.shape),
        ],
        out_specs=[token_block(count, columns), token_block(count, width)],
        out_shape=[
            jax.ShapeDtypeStruct((2, QUADS, count, columns), jnp.bfloat16),
            jax.ShapeDtypeStruct((2, QUADS, count, width), jnp.bfloat16),
        ],
        scratch_shapes=[pltpu.VMEM((2 * count, 2 * count), jnp.float32)],
        cost_estimate=pl.CostEstimate(
            flops=4 * HD * pairs, bytes_accessed=24 * QUADS * count * columns, transcendentals=pairs
        ),
        name="attention",
    )(top, bottom, cosine, sine, marks_row, marks_column)


def attention_back(qkv, grad_mixed, cosine, sine, marks_row, marks_column, shift):
    _, _, count, columns = qkv.shape
    width = columns // 3
    pairs = QUADS * (2 * count) * (2 * count) * (width // HD)
    return pl.pallas_call(
        lambda *refs: attention_back_kernel(shift, *refs),
        grid=(QUADS,),
        in_specs=[
            token_block(count, columns),
            token_block(count, width),
            piece_block(cosine.shape),
            piece_block(sine.shape),
            piece_block(marks_row.shape),
            piece_block(marks_column.shape),
        ],
        out_specs=token_block(count, columns),
        out_shape=jax.ShapeDtypeStruct(qkv.shape, jnp.bfloat16),
        scratch_shapes=[pltpu.VMEM((2 * count, 2 * count), jnp.float32)],
        cost_estimate=pl.CostEstimate(
            flops=10 * HD * pairs, bytes_accessed=12 * QUADS * count * columns, transcendentals=pairs
        ),
        name="attention_back",
    )(qkv, grad_mixed, cosine, sine, marks_row, marks_column)


def plane(
    inputs,
    cotangent,
    segment_ids,
    block_ids,
    positions,
    w_qkv,
    w_out,
    w_gateup,
    w_down,
    gain_attn,
    gain_ffn,
):
    _, _, rows, width = inputs.shape
    length = segment_ids.shape[2]
    shard = w_qkv.shape[0]
    place = lax.axis_index("fsdp")
    column = lax.axis_index("tp")
    core = place % 2
    quad = place // 2
    first = (column % 2) == 0
    shift = -math.log(length)

    def own_first(pair):
        return choose(first, pair[0], pair[1]), choose(first, pair[1], pair[0])

    def half_marks(marks):
        line = choose(first, marks[0, 0], marks[1, 0])
        own = lax.dynamic_slice_in_dim(line, column * rows, rows, 0)
        other = lax.dynamic_slice_in_dim(line, (column ^ 1) * rows, rows, 0)
        return [wide(own), wide(other)]

    small = jnp.concatenate(
        [wide(gain_attn), wide(gain_ffn)]
        + half_marks(segment_ids)
        + half_marks(block_ids)
        + half_marks(positions)
    )
    table = lax.all_gather(small, "fsdp")
    gain_one = table[:, :shard].reshape(width)
    gain_two = table[:, shard : 2 * shard].reshape(width)
    marks = jnp.stack(
        [
            lax.dynamic_index_in_dim(table, place ^ (2 * step), 0, keepdims=False)[2 * shard :]
            for step in range(QUADS)
        ]
    ).reshape(QUADS, 3, 2 * rows)
    marks_row = marks[:, :2]
    marks_column = marks_row.transpose(0, 2, 1)
    ladder = jnp.arange(HD // 2, dtype=jnp.float32) * (2.0 / HD)
    angles = marks[:, 2, :, None] * jnp.exp(-math.log(rope_base) * ladder)
    cosine = jnp.cos(angles)
    sine = jnp.sin(angles)
    cosine = jnp.concatenate([cosine, cosine], axis=-1)
    sine = jnp.concatenate([-sine, sine], axis=-1)

    part_qkv = spread_rows(
        w_qkv.reshape(shard, 3, QUADS, -1).transpose(0, 2, 1, 3).reshape(shard, -1), quad
    )
    full_qkv = gather_columns(part_qkv, core)
    full_out = gather_columns(spread_rows(w_out, quad), core)
    full_gate = gather_columns(spread_rows(w_gateup[:, 0], quad), core)
    full_up = gather_columns(spread_rows(w_gateup[:, 1], quad), core)
    full_down = gather_columns(spread_rows(w_down, quad), core)

    residual = [wide(value) for value in own_first(inputs[:, 0])]
    norm_one = [normalize(value) for value in residual]
    normed_one = [low(unit * gain_one) for unit, _ in norm_one]
    top_one = gather_tokens(normed_one[0])
    bottom_one = gather_tokens(over_pair(normed_one[1]))
    qkv, mixed = attention(
        mm("td,de->te", top_one, full_qkv),
        mm("td,de->te", bottom_one, full_qkv),
        cosine,
        sine,
        marks_row,
        marks_column,
        shift,
    )
    count = QUADS * rows
    mixed_all = mixed.reshape(2 * count, -1)
    term = low(mm("tc,dc->td", mixed_all, full_out))
    other_half = over_pair(low(scatter_tokens(term[count:])))
    own_half = scatter_tokens(term[:count])
    middle = [residual[0] + own_half, residual[1] + wide(other_half)]

    norm_two = [normalize(value) for value in middle]
    normed_two = [low(unit * gain_two) for unit, _ in norm_two]
    grad_top = own_first(cotangent[:, 0])
    results = [None, None]
    grad_middle = [None, None]
    ffn = [None, None]
    gain_two_sum = 0.0
    for side in (1, 0):
        tokens = gather_tokens(normed_two[side])
        tops = gather_tokens(grad_top[side])
        gate = mm("td,df->tf", tokens, full_gate)
        up = mm("td,df->tf", tokens, full_up)
        sigma = jax.nn.sigmoid(gate)
        silu = gate * sigma
        hidden = low(silu * up)
        grad_hidden = mm("td,df->tf", tops, full_down)
        grad_gate = low(grad_hidden * up * sigma * (1.0 + gate * (1.0 - sigma)))
        grad_up = low(grad_hidden * silu)
        back = low(mm("tf,df->td", grad_gate, full_gate) + mm("tf,df->td", grad_up, full_up))
        grad_normed = scatter_tokens(back)
        unit, factor = norm_two[side]
        grad_middle[side] = wide(grad_top[side]) + normalize_back(grad_normed, unit, factor, gain_two)
        gain_two_sum = gain_two_sum + jnp.sum(grad_normed * unit, axis=0)
        results[side] = low(
            middle[side] + scatter_tokens(low(mm("tf,df->td", hidden, full_down)))
        )
        ffn[side] = (tokens, tops, hidden, grad_gate, grad_up)
    tokens_two, tops_all, hidden_all, grad_gate_all, grad_up_all = [
        jnp.concatenate(both, axis=0) for both in zip(*ffn)
    ]
    grad_down = reduce_weight_grad(mm("td,tf->df", tops_all, hidden_all), core, quad)
    grad_gate_rows = reduce_weight_grad(mm("td,tf->df", tokens_two, grad_gate_all), core, quad)
    grad_up_rows = reduce_weight_grad(mm("td,tf->df", tokens_two, grad_up_all), core, quad)

    grad_low = [low(value) for value in grad_middle]
    grad_all = jnp.concatenate(
        [gather_tokens(grad_low[0]), gather_tokens(over_pair(grad_low[1]))], axis=0
    )
    grad_mixed = low(mm("td,dc->tc", grad_all, full_out))
    grad_qkv = attention_back(
        qkv,
        grad_mixed.reshape(mixed.shape),
        cosine,
        sine,
        marks_row,
        marks_column,
        shift,
    ).reshape(2 * count, -1)
    term = low(mm("te,de->td", grad_qkv, full_qkv))
    other_half = over_pair(low(scatter_tokens(term[count:])))
    grad_normed_one = [scatter_tokens(term[:count]), wide(other_half)]
    grad_inputs = [
        grad_middle[side]
        + normalize_back(grad_normed_one[side], norm_one[side][0], norm_one[side][1], gain_one)
        for side in range(2)
    ]
    gain_one_sum = jnp.sum(grad_normed_one[0] * norm_one[0][0], axis=0) + jnp.sum(
        grad_normed_one[1] * norm_one[1][0], axis=0
    )
    grad_out_rows = reduce_weight_grad(mm("td,tc->dc", grad_all, mixed_all), core, quad)
    tokens_one = jnp.concatenate([top_one, bottom_one], axis=0)
    grad_qkv_rows = reduce_weight_grad(mm("td,te->de", tokens_one, grad_qkv), core, quad)
    grad_qkv_rows = (
        grad_qkv_rows.reshape(shard, QUADS, 3, -1).transpose(0, 2, 1, 3).reshape(w_qkv.shape)
    )
    gains = reduce_gain_grads(jnp.stack([gain_one_sum, gain_two_sum]), place)
    return (
        jnp.stack(own_first(results))[:, None],
        jnp.stack(own_first(grad_inputs))[:, None],
        grad_qkv_rows,
        grad_out_rows,
        jnp.stack([grad_gate_rows, grad_up_rows], axis=1),
        grad_down,
        gains[0],
        gains[1],
    )


def solution(mesh):
    body = plane if plane_fits(mesh) else local
    return jax.shard_map(
        body,
        mesh=mesh,
        in_specs=(
            P(None, "fsdp", "tp", None),
            P(None, "fsdp", "tp", None),
            P(None, "fsdp", None),
            P(None, "fsdp", None),
            P(None, "fsdp", None),
            P("fsdp", None, "tp"),
            P("fsdp", "tp"),
            P("fsdp", None, "tp"),
            P("fsdp", "tp"),
            P("fsdp"),
            P("fsdp"),
        ),
        out_specs=(
            P(None, "fsdp", "tp", None),
            P(None, "fsdp", "tp", None),
            P("fsdp", None, "tp"),
            P("fsdp", "tp"),
            P("fsdp", None, "tp"),
            P("fsdp", "tp"),
            P("fsdp"),
            P("fsdp"),
        ),
        check_vma=False,
    )
```
